32 devices in a mesh: seg: 2 (over y), src: 4 (over z), rcv: 2 (over x), frq: 2 (over core).
Axes of the slice: x: 2, y: 2, z: 4, core: 2. Of those that a mesh axis runs over, the one named last changes fastest.
Arguments:
- spectra: bfloat16 [1024, 2, 32, 128], P(('seg', 'src', 'rcv', 'frq')), parts along dimension 0, may hold values from -1000 to 1000
- freq_bins: int32 [16], replicated, may hold values from 0 to 31, as said below
Outputs:
- cross_spectra: bfloat16 [2, 16, 1024, 512], P(None, 'frq', ('seg', 'src'), 'rcv'), parts along dimension 2
The draws below stay inside these ranges and needn't reach their ends.
There are 2 independent parts, one for each index of `seg`. The reference program is written for one: setup_inputs(seed, part) draws one part's arguments, and reference() takes and returns one part's arrays. A program takes and returns all parts, laid end to end along the dimension named above; an argument that names none is the same for every part. Nothing has to cross between parts.
Inputs may be any that keep to these rules, and one draw needn't show every extreme that they name: `freq_bins`: distinct and increasing.
All inputs are finite; a program needn't handle non-finite values.
Results may differ from the reference program's by a relative error of at most 0.0057.
Values may be sent and summed in bfloat16 or wider, within the bound.
No kernel may reach another device: no remote copies, remote signals or barrier semaphores. Data moves between devices by JAX's collectives and lax.ppermute only.
A program may use at most 64 MiB of HBM per device.

```python
import math
import jax
import jax.numpy as jnp
from jax import lax

F = 16
NB = 32
W = 128
CHANNELS = 512


def draw_spectra(key, part):
    key_base = jax.random.fold_in(key, 11)
    key_rows = jax.random.fold_in(key, 12)
    key_bins = jax.random.fold_in(key, 13)
    shape = (CHANNELS, 2, NB, W)
    row_scale = jnp.exp(jax.random.uniform(key_rows, (CHANNELS, 1, 1, W), jnp.float32, 0.0, math.log(10.0)))
    bin_scale = jnp.exp(jax.random.uniform(key_bins, (1, 1, NB, 1), jnp.float32, 0.0, math.log(10.0)))
    base = jnp.clip(jax.random.normal(key_base, shape, jnp.float32), -6.0, 6.0)
    return (base * row_scale * bin_scale).astype(jnp.bfloat16)


def draw_freq_bins(key, part):
    inner = jax.random.permutation(jax.random.fold_in(key, 21), jnp.arange(1, NB - 1, dtype=jnp.int32))
    picked = jnp.concatenate([jnp.array([0, NB - 1], dtype=jnp.int32), inner[:F - 2]])
    return jnp.sort(picked).astype(jnp.int32)


def setup_inputs(seed: int = 0, part: int = 0) -> dict:
    keys = jax.random.split(jax.random.key(seed), 3)
    part_keys = jax.random.split(jax.random.fold_in(keys[2], part), 3)
    return {
        "spectra": draw_spectra(jax.random.fold_in(jax.random.fold_in(keys[2], part), 71), part),
        "freq_bins": draw_freq_bins(jax.random.fold_in(keys[2], 71), part),
    }


def reference(spectra, freq_bins):
    values = spectra.astype(jnp.float32)
    band_power = lax.optimization_barrier(jnp.mean(values * values, axis=(1, 2)))
    inverse_rms = lax.rsqrt(band_power + 1e-06)
    picker = (freq_bins[:, None] == jnp.arange(NB, dtype=jnp.int32)[None, :]).astype(jnp.float32)
    chosen = jnp.einsum('fb,crbw->rfcw', picker, values)
    whitened = (chosen * inverse_rms[None, None]).astype(jnp.bfloat16)
    factor = 1.0 / math.sqrt(W)

    def one_bin(layer):
        real_part = jnp.dot(layer[0], layer[0].T, preferred_element_type=jnp.float32) + jnp.dot(layer[1], layer[1].T, preferred_element_type=jnp.float32)
        imag_part = jnp.dot(layer[0], layer[1].T, preferred_element_type=jnp.float32) - jnp.dot(layer[1], layer[0].T, preferred_element_type=jnp.float32)
        return (jnp.stack([real_part, imag_part]) * factor).astype(jnp.bfloat16)
    stacked = lax.map(one_bin, jnp.transpose(whitened, (1, 0, 2, 3)))
    return jnp.transpose(stacked, (1, 0, 2, 3))
```

```python
import functools
import math

import jax
import jax.numpy as jnp
from jax import lax
from jax.experimental import pallas as pl
from jax.experimental.pallas import tpu as pltpu
from jax.sharding import PartitionSpec as P

AXES = ("src", "rcv", "frq")


def whiten_kernel(cores, bins_ref, x_ref, *refs):
    chunk_refs, wide = refs[:cores], refs[cores]
    bins_here, channels, depth = chunk_refs[0].shape
    windows = depth // 2
    rows = wide.shape[0] // channels
    band = rows // 2
    wide[...] = x_ref[...].astype(jnp.float32)
    power = jnp.zeros((channels, windows), jnp.float32)
    for row in range(rows):
        part = wide[pl.ds(row, channels, stride=rows), :]
        power = power + part * part
    inverse_rms = lax.rsqrt(power * (1.0 / rows) + 1e-06)
    core = lax.axis_index("frq")
    for shift in range(cores):
        owner = lax.rem(core + shift, cores)
        for f in range(bins_here):
            picked = bins_ref[owner * bins_here + f]
            for part in range(2):
                values = wide[pl.ds(part * band + picked, channels, stride=rows), :]
                chunk_refs[shift][f, :, part * windows : (part + 1) * windows] = (
                    values * inverse_rms
                ).astype(jnp.bfloat16)


def whiten(spectra, freq_bins):
    channels, parts, band, windows = spectra.shape
    cores = lax.axis_size("frq")
    chunk = jax.ShapeDtypeStruct(
        (freq_bins.shape[0] // cores, channels, parts * windows), jnp.bfloat16
    )
    return pl.pallas_call(
        functools.partial(whiten_kernel, cores),
        out_shape=[chunk] * cores,
        in_specs=[
            pl.BlockSpec(memory_space=pltpu.SMEM),
            pl.BlockSpec(memory_space=pltpu.VMEM),
        ],
        out_specs=[pl.BlockSpec(memory_space=pltpu.VMEM)] * cores,
        scratch_shapes=[pltpu.VMEM((channels * parts * band, windows), jnp.float32)],
        name="whiten",
    )(freq_bins, spectra.reshape(channels * parts * band, windows))


def spot():
    columns = lax.axis_size("rcv")
    groups = lax.axis_size("src") // columns
    s = lax.axis_index("src")
    return lax.axis_index("rcv"), s // groups, lax.rem(s, groups), lax.axis_index("frq")


def product_kernel(source_of, receiver_of, step, n_in, aliased, *refs):
    ins, rest = refs[:n_in], refs[n_in:]
    out_ref, left, right, result, sems = rest[1:] if aliased else rest
    columns, cores = lax.axis_size("rcv"), lax.axis_size("frq")
    groups = lax.axis_size("src") // columns
    column, half, place, core = spot()
    channels = ins[0].shape[1]
    bins_here, rows, depth = left.shape
    windows = depth // 2

    def fill(target, entries):
        for index, valid, unit, shift in entries:
            owner = lax.rem(core + cores - shift, cores)
            start = pl.multiple_of((unit * cores + owner) * channels, channels)

            def store(index=index, start=start):
                target[:, pl.ds(start, channels), :] = ins[index][...]

            if valid is None:
                store()
            else:
                pl.when(valid)(store)

    fill(left, source_of(column, half, columns))
    fill(right, receiver_of(column, half, columns))
    block = lax.rem(place + groups - step, groups)
    factor = 1.0 / math.sqrt(windows)
    copies = []
    for f in range(bins_here):
        both = left[f]
        turned = jnp.concatenate([-both[:, windows:], both[:, :windows]], axis=1)
        product = lax.dot_general(
            jnp.concatenate([both, turned], axis=0),
            right[f],
            (((1,), (1,)), ((), ())),
            preferred_element_type=jnp.float32,
        )
        result[f] = (product * factor).astype(jnp.bfloat16).reshape(2, rows, rows)
        for part in range(2):
            copy = pltpu.make_async_copy(
                result.at[f, part],
                out_ref.at[part, f, :, pl.ds(pl.multiple_of(block * rows, rows), rows)],
                sems.at[f, part],
            )
            copy.start()
            copies.append(copy)
    for copy in copies:
        copy.wait()


def products(step, chunks, source_of, receiver_of, previous, out_shape):
    bins_here, channels, depth = chunks[0].shape
    rows = out_shape[2]
    operands = list(chunks)
    in_specs = [pl.BlockSpec(memory_space=pltpu.VMEM)] * len(chunks)
    aliases = {}
    if previous is not None:
        aliases = {len(operands): 0}
        operands.append(previous)
        in_specs.append(pl.BlockSpec(memory_space=pl.ANY))
    return pl.pallas_call(
        functools.partial(
            product_kernel, source_of, receiver_of, step, len(chunks), previous is not None
        ),
        out_shape=jax.ShapeDtypeStruct(out_shape, jnp.bfloat16),
        in_specs=in_specs,
        out_specs=pl.BlockSpec(memory_space=pl.ANY),
        scratch_shapes=[
            pltpu.VMEM((bins_here, rows, depth), jnp.bfloat16),
            pltpu.VMEM((bins_here, rows, depth), jnp.bfloat16),
            pltpu.VMEM((bins_here, 2, rows, rows), jnp.bfloat16),
            pltpu.SemaphoreType.DMA((bins_here, 2)),
        ],
        input_output_aliases=aliases,
        name=f"products{step}",
    )(*operands)


def local(spectra, freq_bins):
    columns, cores = lax.axis_size("rcv"), lax.axis_size("frq")
    groups = lax.axis_size("src") // columns

    def permute(value, moves):
        pairs = []
        for (x, h, g), (tx, th, tg) in moves:
            for core in range(cores):
                here = ((h * groups + g) * columns + x) * cores + core
                there = ((th % columns * groups + tg % groups) * columns + tx % columns) * cores
                pairs.append((here, there + core))
        return lax.ppermute(value, AXES, pairs)

    halves, places = range(columns), range(groups)
    heavies = range(1, columns)

    def first(value, d):
        moves = []
        for h in halves:
            for g in places:
                moves.append(((h, h, g), (h, h + d, g)))
                moves.append((((h - d) % columns, h, g), (h, h, g)))
        return permute(value, moves)

    def second(value, k):
        moves = []
        for h in halves:
            for g in places:
                if k < columns - 1:
                    for d in heavies:
                        to = 1 + (d - 1 + k) % (columns - 1)
                        moves.append((((h - d) % columns, h, g), (h, h + to, g)))
                if k < groups - 1:
                    moves.append(((h, h, g), (h, h, g + k + 1)))
        return permute(value, moves)

    def third(value, d):
        moves = []
        for h in halves:
            for g in places:
                for x in range(columns):
                    if (x + d) % columns != h:
                        moves.append(((x, h, g), (x + d, h, g)))
        return permute(value, moves)

    def onward(value, step, light, heavy):
        moves = []
        for h in halves:
            for g in places:
                for x in range(columns):
                    if (light if x == h else heavy((h - x) % columns)):
                        moves.append(((x, h, g), (x, h, g + step)))
        return permute(value, moves)

    made = whiten(spectra, freq_bins)
    own = [made[0]]
    ones, twos, threes = {}, {}, {}
    for shift in range(cores):
        if shift:
            pairs = [(c, (c + shift) % cores) for c in range(cores)]
            own.append(lax.ppermute(made[shift], "frq", pairs))
        for k in range(max(columns, groups) - 1):
            twos[k, shift] = second(own[shift], k)
        for d in heavies:
            ones[d, shift] = first(own[shift], d)
    for shift in range(cores):
        for d in heavies:
            threes[d, shift] = third(own[shift], d)

    def pack(entries):
        values = [value for value, *_ in entries]
        return values, [(i, *entry[1:]) for i, entry in enumerate(entries)]

    base = [(own[c], c) for c in range(cores)]
    base += [(ones[d, c], c) for d in heavies for c in range(cores)]
    base += [(threes[d, c], c) for d in heavies for c in range(cores)]

    def source_of(column, half, columns):
        light = column == half
        entries = [(c, None, column, c) for c in range(cores)]
        at = cores
        for d in heavies:
            for c in range(cores):
                entries.append((at, light, lax.rem(column + columns - d, columns), c))
                at += 1
        for d in heavies:
            unit = lax.rem(column + columns - d, columns)
            for c in range(cores):
                entries.append((at, jnp.logical_not(light), unit, c))
                at += 1
        return entries

    def heavy_unit(column, half, columns, k):
        d = lax.rem(half + columns - column, columns)
        back = 1 + lax.rem(d - 1 - k + 2 * (columns - 1), columns - 1)
        return lax.rem(column + columns - back, columns)

    rows = spectra.shape[0] * cores * columns
    out_shape = (2, own[0].shape[0], rows, rows * groups)
    out = None
    for step in range(groups):
        chunks = [value for value, _ in base]
        lights, firsts, seconds = [], [], []
        for c in range(cores):
            if step:
                lights.append((len(chunks), c))
                chunks.append(twos[step - 1, c])
            else:
                lights.append((c, c))
        for d in heavies:
            for c in range(cores):
                if step:
                    value = onward(ones[d, c], step, True, lambda e, d=d: e == d)
                    firsts.append((len(chunks), d, c))
                    chunks.append(value)
                else:
                    firsts.append((cores + (d - 1) * cores + c, d, c))
        for k in range(columns - 1):
            for c in range(cores):
                value = twos[k, c]
                if step:
                    value = onward(value, step, False, lambda e: True)
                seconds.append((len(chunks), k, c))
                chunks.append(value)

        def receiver_of(column, half, columns, lights=lights, firsts=firsts, seconds=seconds):
            light = column == half
            heavy = jnp.logical_not(light)
            entries = [(i, light, column, c) for i, c in lights]
            for i, d, c in firsts:
                beside = lax.rem(column + columns - d, columns)
                mine = lax.rem(column + d, columns) == half
                entries.append((i, light, beside, c))
                entries.append((i, mine, column, c))
            for i, k, c in seconds:
                entries.append((i, heavy, heavy_unit(column, half, columns, k), c))
            return entries

        out = products(step, chunks, source_of, receiver_of, out, out_shape)
    return out


def solution(mesh):
    in_specs = (P(("seg", "src", "rcv", "frq"), None, None, None), P())
    out_specs = P(None, "frq", ("seg", "src"), "rcv")
    return jax.shard_map(local, mesh=mesh, in_specs=in_specs, out_specs=out_specs, check_vma=False)
```

```python
import functools
import math

import jax
import jax.numpy as jnp
from jax import lax
from jax.experimental import pallas as pl
from jax.experimental.pallas import tpu as pltpu
from jax.sharding import PartitionSpec as P

AXES = ("src", "rcv", "frq")


def whiten_kernel(cores, bins_ref, x_ref, *refs):
    chunk_refs, wide = refs[:cores], refs[cores]
    bins_here, channels, depth = chunk_refs[0].shape
    windows = depth // 2
    rows = wide.shape[0] // channels
    band = rows // 2
    wide[...] = x_ref[...].astype(jnp.float32)
    power = jnp.zeros((channels, windows), jnp.float32)
    for row in range(rows):
        part = wide[pl.ds(row, channels, stride=rows), :]
        power = power + part * part
    inverse_rms = lax.rsqrt(power * (1.0 / rows) + 1e-06)
    core = lax.axis_index("frq")
    for shift in range(cores):
        owner = lax.rem(core + shift, cores)
        for f in range(bins_here):
            picked = bins_ref[owner * bins_here + f]
            for part in range(2):
                values = wide[pl.ds(part * band + picked, channels, stride=rows), :]
                chunk_refs[shift][f, :, part * windows : (part + 1) * windows] = (
                    values * inverse_rms
                ).astype(jnp.bfloat16)


def whiten(spectra, freq_bins):
    channels, parts, band, windows = spectra.shape
    cores = lax.axis_size("frq")
    chunk = jax.ShapeDtypeStruct(
        (freq_bins.shape[0] // cores, channels, parts * windows), jnp.bfloat16
    )
    return pl.pallas_call(
        functools.partial(whiten_kernel, cores),
        out_shape=[pltpu.VMEM(chunk.shape, chunk.dtype)] * cores,
        in_specs=[
            pl.BlockSpec(memory_space=pltpu.SMEM),
            pl.BlockSpec(memory_space=pltpu.VMEM),
        ],
        out_specs=[pl.BlockSpec(memory_space=pltpu.VMEM)] * cores,
        scratch_shapes=[pltpu.VMEM((channels * parts * band, windows), jnp.float32)],
        name="whiten",
    )(freq_bins, spectra.reshape(channels * parts * band, windows))


def spot():
    columns = lax.axis_size("rcv")
    groups = lax.axis_size("src") // columns
    s = lax.axis_index("src")
    return lax.axis_index("rcv"), s // groups, lax.rem(s, groups), lax.axis_index("frq")


def product_kernel(source_of, receiver_of, step, n_in, aliased, *refs):
    ins, rest = refs[:n_in], refs[n_in:]
    out_ref, left, right, result, sems = rest[1:] if aliased else rest
    columns, cores = lax.axis_size("rcv"), lax.axis_size("frq")
    groups = lax.axis_size("src") // columns
    column, half, place, core = spot()
    channels = ins[0].shape[1]
    bins_here, rows, depth = left.shape
    windows = depth // 2

    def fill(target, entries):
        for index, valid, unit, shift in entries:
            owner = lax.rem(core + cores - shift, cores)
            start = pl.multiple_of((unit * cores + owner) * channels, channels)

            def store(index=index, start=start):
                target[:, pl.ds(start, channels), :] = ins[index][...]

            if valid is None:
                store()
            else:
                pl.when(valid)(store)

    fill(left, source_of(column, half, columns))
    fill(right, receiver_of(column, half, columns))
    block = lax.rem(place + groups - step, groups)
    factor = 1.0 / math.sqrt(windows)
    copies = []
    for f in range(bins_here):
        both = left[f]
        turned = jnp.concatenate([-both[:, windows:], both[:, :windows]], axis=1)
        product = lax.dot_general(
            jnp.concatenate([both, turned], axis=0),
            right[f],
            (((1,), (1,)), ((), ())),
            preferred_element_type=jnp.float32,
        )
        result[f] = (product * factor).astype(jnp.bfloat16).reshape(2, rows, rows)
        for part in range(2):
            copy = pltpu.make_async_copy(
                result.at[f, part],
                out_ref.at[part, f, :, pl.ds(pl.multiple_of(block * rows, rows), rows)],
                sems.at[f, part],
            )
            copy.start()
            copies.append(copy)
    for copy in copies:
        copy.wait()


def products(step, chunks, source_of, receiver_of, previous, out_shape):
    bins_here, channels, depth = chunks[0].shape
    rows = out_shape[2]
    operands = [pltpu.with_memory_space_constraint(c, pltpu.VMEM) for c in chunks]
    in_specs = [pl.BlockSpec(memory_space=pltpu.VMEM)] * len(chunks)
    aliases = {}
    if previous is not None:
        aliases = {len(operands): 0}
        operands.append(previous)
        in_specs.append(pl.BlockSpec(memory_space=pl.ANY))
    return pl.pallas_call(
        functools.partial(
            product_kernel, source_of, receiver_of, step, len(chunks), previous is not None
        ),
        out_shape=jax.ShapeDtypeStruct(out_shape, jnp.bfloat16),
        in_specs=in_specs,
        out_specs=pl.BlockSpec(memory_space=pl.ANY),
        scratch_shapes=[
            pltpu.VMEM((bins_here, rows, depth), jnp.bfloat16),
            pltpu.VMEM((bins_here, rows, depth), jnp.bfloat16),
            pltpu.VMEM((bins_here, 2, rows, rows), jnp.bfloat16),
            pltpu.SemaphoreType.DMA((bins_here, 2)),
        ],
        input_output_aliases=aliases,
        name=f"products{step}",
    )(*operands)


def local(spectra, freq_bins):
    columns, cores = lax.axis_size("rcv"), lax.axis_size("frq")
    groups = lax.axis_size("src") // columns

    def permute(value, moves):
        pairs = []
        for (x, h, g), (tx, th, tg) in moves:
            for core in range(cores):
                here = ((h * groups + g) * columns + x) * cores + core
                there = ((th % columns * groups + tg % groups) * columns + tx % columns) * cores
                pairs.append((here, there + core))
        return lax.ppermute(value, AXES, pairs)

    halves, places = range(columns), range(groups)
    heavies = range(1, columns)

    def first(value, d):
        moves = []
        for h in halves:
            for g in places:
                moves.append(((h, h, g), (h, h + d, g)))
                moves.append((((h - d) % columns, h, g), (h, h, g)))
        return permute(value, moves)

    def second(value, k):
        moves = []
        for h in halves:
            for g in places:
                if k < columns - 1:
                    for d in heavies:
                        to = 1 + (d - 1 + k) % (columns - 1)
                        moves.append((((h - d) % columns, h, g), (h, h + to, g)))
                if k < groups - 1:
                    moves.append(((h, h, g), (h, h, g + k + 1)))
        return permute(value, moves)

    def third(value, d):
        moves = []
        for h in halves:
            for g in places:
                for x in range(columns):
                    if (x + d) % columns != h:
                        moves.append(((x, h, g), (x + d, h, g)))
        return permute(value, moves)

    def onward(value, step, light, heavy):
        moves = []
        for h in halves:
            for g in places:
                for x in range(columns):
                    if (light if x == h else heavy((h - x) % columns)):
                        moves.append(((x, h, g), (x, h, g + step)))
        return permute(value, moves)

    made = whiten(spectra, freq_bins)
    own = [made[0]]
    ones, twos, threes = {}, {}, {}
    for shift in range(cores):
        if shift:
            pairs = [(c, (c + shift) % cores) for c in range(cores)]
            own.append(lax.ppermute(made[shift], "frq", pairs))
        for k in range(max(columns, groups) - 1):
            twos[k, shift] = second(own[shift], k)
        for d in heavies:
            ones[d, shift] = first(own[shift], d)
    for shift in range(cores):
        for d in heavies:
            threes[d, shift] = third(own[shift], d)

    def pack(entries):
        values = [value for value, *_ in entries]
        return values, [(i, *entry[1:]) for i, entry in enumerate(entries)]

    base = [(own[c], c) for c in range(cores)]
    base += [(ones[d, c], c) for d in heavies for c in range(cores)]
    base += [(threes[d, c], c) for d in heavies for c in range(cores)]

    def source_of(column, half, columns):
        light = column == half
        entries = [(c, None, column, c) for c in range(cores)]
        at = cores
        for d in heavies:
            for c in range(cores):
                entries.append((at, light, lax.rem(column + columns - d, columns), c))
                at += 1
        for d in heavies:
            unit = lax.rem(column + columns - d, columns)
            for c in range(cores):
                entries.append((at, jnp.logical_not(light), unit, c))
                at += 1
        return entries

    def heavy_unit(column, half, columns, k):
        d = lax.rem(half + columns - column, columns)
        back = 1 + lax.rem(d - 1 - k + 2 * (columns - 1), columns - 1)
        return lax.rem(column + columns - back, columns)

    rows = spectra.shape[0] * cores * columns
    out_shape = (2, own[0].shape[0], rows, rows * groups)
    out = None
    for step in range(groups):
        chunks = [value for value, _ in base]
        lights, firsts, seconds = [], [], []
        for c in range(cores):
            if step:
                lights.append((len(chunks), c))
                chunks.append(twos[step - 1, c])
            else:
                lights.append((c, c))
        for d in heavies:
            for c in range(cores):
                if step:
                    value = onward(ones[d, c], step, True, lambda e, d=d: e == d)
                    firsts.append((len(chunks), d, c))
                    chunks.append(value)
                else:
                    firsts.append((cores + (d - 1) * cores + c, d, c))
        for k in range(columns - 1):
            for c in range(cores):
                value = twos[k, c]
                if step:
                    value = onward(value, step, False, lambda e: True)
                seconds.append((len(chunks), k, c))
                chunks.append(value)

        def receiver_of(column, half, columns, lights=lights, firsts=firsts, seconds=seconds):
            light = column == half
            heavy = jnp.logical_not(light)
            entries = [(i, light, column, c) for i, c in lights]
            for i, d, c in firsts:
                beside = lax.rem(column + columns - d, columns)
                mine = lax.rem(column + d, columns) == half
                entries.append((i, light, beside, c))
                entries.append((i, mine, column, c))
            for i, k, c in seconds:
                entries.append((i, heavy, heavy_unit(column, half, columns, k), c))
            return entries

        out = products(step, chunks, source_of, receiver_of, out, out_shape)
    return out


def solution(mesh):
    in_specs = (P(("seg", "src", "rcv", "frq"), None, None, None), P())
    out_specs = P(None, "frq", ("seg", "src"), "rcv")
    return jax.shard_map(local, mesh=mesh, in_specs=in_specs, out_specs=out_specs, check_vma=False)
```
